32 devices in a mesh: fsdp: 16 (over z, y, x), mp: 2 (over core).
Axes of the slice: x: 2, y: 2, z: 4, core: 2. Of those that a mesh axis runs over, the one named last changes fastest.
Arguments:
- first_moment: float32 [1, 16, 32, 128, 1024], P(None, None, 'fsdp', 'mp'), may hold values from -20 to 20
- second_moment: float32 [1, 16, 32, 128, 1024], P(None, None, 'fsdp', 'mp'), may hold values from 0.0005 to 20
- parity_groups: int32 [2, 16], replicated, may hold values from 0 to 3, as said below
Outputs:
- first_quant: bfloat16 [1, 4096, 128, 128], P(None, ('fsdp', 'mp'))
- second_quant: bfloat16 [1, 4096, 128, 128], P(None, ('fsdp', 'mp'))
- first_scale: float32 [1, 4096], P(None, ('fsdp', 'mp'))
- second_scale: float32 [1, 4096], P(None, ('fsdp', 'mp'))
- parity: float32 [32, 2, 1, 128, 128, 128], P(('fsdp', 'mp'))
The draws below stay inside these ranges and needn't reach their ends.
Inputs may be any that keep to these rules, and one draw needn't show every extreme that they name: `parity_groups`: each row is never falling along fsdp, starts at 0 and names all 4 groups; every group of a row holds 1 to 8 consecutive shards, some group holds exactly 8, and the last group holds only the last shard.
All inputs are finite; a program needn't handle non-finite values. Where the reference program divides by a largest or mean magnitude, that divisor is 1e-20 or more.
Results may differ from the reference program's by a relative error of at most 0.005.
Values may be sent and summed in bfloat16 or wider, within the bound.
No kernel may reach another device: no remote copies, remote signals or barrier semaphores. Data moves between devices by JAX's collectives and lax.ppermute only.
A program may use at most 128 MiB of HBM per device.

```python
import jax
import jax.numpy as jnp
from jax import lax

D = 1024
LAYERS = 1
BLK = 128
PB = 32
QB = 16
NBC = 8
NBLK = 4096
SHARDS = 32
BPD = 128
MP_DEV = 2
FS_DEV = 16
GROUPS = 4


def draw_first_moment(key, part):
    base_key = jax.random.fold_in(jax.random.fold_in(key, 11), 0)
    shape = (LAYERS, QB, PB, BLK, D)
    values = jnp.clip(jax.random.normal(base_key, shape), -6.0, 6.0)
    return values.astype(jnp.float32)


def draw_second_moment(key, part):
    base_key = jax.random.fold_in(jax.random.fold_in(key, 23), 0)
    shape = (LAYERS, QB, PB, BLK, D)
    normal = jnp.clip(jax.random.normal(base_key, shape), -6.0, 6.0)
    values = 0.01 + 0.5 * normal * normal
    return values.astype(jnp.float32)


def group_row(key):
    pick_key, fill_key = jax.random.split(key)
    slots = jnp.arange(GROUPS - 1, dtype=jnp.int32)
    widest = jax.random.randint(pick_key, (), 0, GROUPS - 1, dtype=jnp.int32)
    sizes = jnp.where(slots == widest, 8, 1).astype(jnp.int32)
    extra = FS_DEV - 1 - 8 - (GROUPS - 2)

    def add_one(step, current):
        scores = jax.random.randint(jax.random.fold_in(fill_key, step), (GROUPS - 1,), 0, 1 << 20, dtype=jnp.int32)
        scores = jnp.where(current < 8, scores, -1)
        chosen = jnp.argmax(scores).astype(jnp.int32)
        return current + (slots == chosen).astype(jnp.int32)
    sizes = lax.fori_loop(0, extra, add_one, sizes)
    ends = jnp.cumsum(sizes).astype(jnp.int32)
    position = jnp.arange(FS_DEV, dtype=jnp.int32)
    labels = jnp.sum((ends[None, :] <= position[:, None]).astype(jnp.int32), axis=1)
    return labels.astype(jnp.int32)


def draw_parity_groups(key, part):
    row_keys = jax.random.split(jax.random.fold_in(key, 37), MP_DEV)
    return jax.vmap(group_row)(row_keys).astype(jnp.int32)


def setup_inputs(seed: int = 0) -> dict:
    seeds = jax.random.split(jax.random.key(seed), 4)
    return {
        "first_moment": draw_first_moment(jax.random.fold_in(seeds[3], 71), 0),
        "second_moment": draw_second_moment(jax.random.fold_in(seeds[3], 71), 0),
        "parity_groups": draw_parity_groups(jax.random.fold_in(seeds[3], 71), 0),
    }


epsilon = 1e-6


def to_blocks(values):
    split = values.reshape(LAYERS, QB, PB, BLK, NBC, BLK)
    moved = split.transpose(0, 4, 1, 2, 3, 5)
    return moved.reshape(LAYERS, NBLK, BLK, BLK)


def quantize(blocks):
    scale = jnp.max(jnp.abs(blocks), axis=(2, 3)) + epsilon
    return (blocks / scale[:, :, None, None]).astype(jnp.bfloat16), scale


def reference(first_moment, second_moment, parity_groups):
    first_quant, first_scale = quantize(to_blocks(first_moment))
    second_quant, second_scale = quantize(to_blocks(second_moment))
    shards = jnp.stack([first_quant.astype(jnp.float32), second_quant.astype(jnp.float32)])
    shards = shards.reshape(2, LAYERS, SHARDS, BPD, BLK, BLK).transpose(2, 0, 1, 3, 4, 5)
    index = jnp.arange(SHARDS, dtype=jnp.int32)
    fsdp_of = index // MP_DEV
    model_of = index % MP_DEV
    group_of = parity_groups[model_of, fsdp_of]
    before_group = parity_groups[model_of, (fsdp_of + FS_DEV - 1) % FS_DEV]
    leading = (fsdp_of == 0) | (group_of != before_group)
    member = leading[:, None] & (model_of[:, None] == model_of[None, :]) & (group_of[None, :] == before_group[:, None])
    weights = member.astype(jnp.float32)
    flat = shards.reshape(SHARDS, 2 * LAYERS * BPD * BLK * BLK)
    parity = jnp.dot(weights, flat, precision=lax.Precision.HIGHEST).reshape(shards.shape)
    return first_quant, second_quant, first_scale, second_scale, parity
```

```python
import functools

import jax
import jax.numpy as jnp
from jax import lax
from jax.experimental import pallas as pl
from jax.experimental.pallas import tpu as pltpu
from jax.sharding import PartitionSpec as P

BLK = 128
STEP = 1
epsilon = 1e-06


def quantise_body(sizes, pos, groups, x_ref, *rest):
    (M, Z, S, BH, cols, PL, r) = sizes
    others, outs = rest[: M - 1], rest[M - 1 : M - 1 + Z]
    scale_ref, held = rest[M - 1 + Z], rest[M + Z]
    bh, qq = pl.program_id(0), pl.program_id(1)
    mine, outer = pos[0], pos[1]
    parts = [(x_ref, mine)] + [(o, lax.rem(mine + M - 1 - i, M)) for i, o in enumerate(others)]
    for p in range(PL):
        for c in range(cols):
            lanes = slice(c * BLK, (c + 1) * BLK)
            peak = jnp.abs(x_ref[p, :, lanes])
            for o in others:
                peak = jnp.maximum(peak, jnp.abs(o[p, :, lanes]))
            scale = jnp.max(peak, axis=(0, 1), keepdims=True) + epsilon
            inverse = 1.0 / scale
            for ref, part in parts:
                held[c * BH + bh, qq, p, part] = (ref[p, :, lanes] * inverse).astype(jnp.bfloat16)
            scale_ref[p, c : c + 1, :] = jnp.broadcast_to(scale, (1, BLK))

    @pl.when((bh == BH - 1) & (qq == r - 1))
    def _():
        F = Z * S
        for d in range(Z):
            z = lax.rem(outer + d, Z)
            outs[d][0:S] = held[pl.ds(z * S, S)]
            last = lax.rem(z * S + F - 1, F)
            ident = groups[mine, last]
            low = lax.fori_loop(
                0, F, lambda e, n: n + jnp.where(groups[mine, e] < ident, 1, 0), jnp.int32(0)
            )
            for q in range(r):
                for p in range(PL):
                    for part in range(M):
                        total = lax.fori_loop(
                            low,
                            last + 1,
                            lambda e, t: t + held[e, q, p, part].astype(jnp.float32),
                            jnp.zeros(held.shape[-2:], jnp.float32),
                        )
                        outs[d][S, q, p, part] = total.astype(jnp.bfloat16)


def parity_body(sizes, pos, groups, *refs):
    (Z, S) = sizes
    came, outs = refs[:Z], refs[Z:]
    mine, outer, inner = pos[0], pos[1], pos[2]
    F = Z * S
    base = outer * S
    entering = groups[mine, lax.rem(base + F - 1, F)]
    weights = []
    for d in range(S):
        j = inner ^ d
        f = base + j
        before = groups[mine, lax.rem(f + F - 1, F)]
        lead = (f == 0) | (groups[mine, f] != before)
        row = [
            jnp.where(lead & (e < j) & (groups[mine, base + e] == before), 1.0, 0.0)
            for e in range(S)
        ]
        row.append(jnp.where(lead & (entering == before), 1.0, 0.0))
        weights.append(row)
    rows = came[0].shape[-2]
    slab = min(rows, 32)
    for dz in range(Z):
        z = lax.rem(outer + Z - dz, Z)
        for d in range(S):
            outs[d][z, 0] = came[dz][inner ^ d]
        for k in range(rows // slab):
            at = slice(k * slab, (k + 1) * slab)
            terms = [came[dz][e, at, :].astype(jnp.float32) for e in range(S + 1)]
            for d in range(S):
                total = weights[d][S] * terms[S]
                for e in range(S):
                    total = total + weights[d][e] * terms[e]
                outs[d][z, 1, at, :] = total.astype(jnp.bfloat16)


def place_body(S, aliased, pos, *refs):
    came = refs[:S]
    quant_ref, parity_ref = refs[S + aliased], refs[S + aliased + 1]
    inner = pos[2]
    for d in range(S):
        quant_ref[inner ^ d] = came[d][0]
        parity_ref[inner ^ d] = came[d][1].astype(jnp.float32)


def shards(first_moment, second_moment, parity_groups):
    L, row_sets, PL, rows, columns = first_moment.shape
    F, M = lax.axis_size("fsdp"), lax.axis_size("mp")
    cols = columns // BLK
    R = row_sets * cols // (F * M)
    BH = row_sets // R // M
    S = 1 << ((F.bit_length() - 1) // 2)
    Z = F // S
    assert F == cols * BH and S % BH == 0 and rows * M == BLK
    r = STEP if R % STEP == 0 else R
    here = lax.axis_index("fsdp")
    mine = lax.axis_index("mp")
    pos = jnp.stack([mine, here // S, here % S]).astype(jnp.int32)
    groups = parity_groups
    moments = [v.reshape(L, BH, M, R, PL, rows, columns) for v in (first_moment, second_moment)]
    chunks = [(a, l, q) for l in range(L) for q in range(0, R, r) for a in range(2)]
    bf16, f32 = jnp.bfloat16, jnp.float32
    zero = lambda *_: (0,)

    def quantise(chunk):
        a, l, q0 = chunk
        x = moments[a][l]
        others = []
        for dd in range(1, M):
            piece = lax.dynamic_index_in_dim(
                x[:, :, q0 : q0 + r], lax.rem(mine + dd, M), axis=1, keepdims=False
            )
            others.append(lax.ppermute(piece, "mp", [(i, (i + dd) % M) for i in range(M)]))
        out_shape = (S + 1, r, PL, M, rows, BLK)
        results = pl.pallas_call(
            functools.partial(quantise_body, (M, Z, S, BH, cols, PL, r)),
            grid_spec=pltpu.PrefetchScalarGridSpec(
                num_scalar_prefetch=2,
                grid=(BH, r),
                in_specs=[
                    pl.BlockSpec(
                        (None, None, None, PL, rows, columns),
                        lambda b, q, pos, groups: (b, pos[0], q0 + q, 0, 0, 0),
                    )
                ]
                + [
                    pl.BlockSpec(
                        (None, None, PL, rows, columns), lambda b, q, pos, groups: (b, q, 0, 0, 0)
                    )
                ]
                * (M - 1),
                out_specs=[pl.BlockSpec(out_shape, lambda b, q, pos, groups: (0,) * 6)] * Z
                + [
                    pl.BlockSpec(
                        (None, None, PL, cols, BLK), lambda b, q, pos, groups: (b, q, 0, 0, 0)
                    )
                ],
                scratch_shapes=[pltpu.VMEM((F, r, PL, M, rows, BLK), bf16)],
            ),
            out_shape=[jax.ShapeDtypeStruct(out_shape, bf16)] * Z
            + [jax.ShapeDtypeStruct((BH, r, PL, cols, BLK), f32)],
            name="quantise",
        )(pos, groups, x, *others)
        return [v.reshape(S + 1, r, PL, BLK, BLK) for v in results[:Z]], results[Z][..., 0]

    def across(pieces):
        return [pieces[0]] + [
            lax.ppermute(
                pieces[d],
                "fsdp",
                [(z * S + j, ((z + d) % Z) * S + j) for z in range(Z) for j in range(S)],
            )
            for d in range(1, Z)
        ]

    def combine(came):
        out_shape = (Z, 2, r, PL, BLK, BLK)
        return pl.pallas_call(
            functools.partial(parity_body, (Z, S)),
            grid_spec=pltpu.PrefetchScalarGridSpec(
                num_scalar_prefetch=2,
                grid=(r, PL),
                in_specs=[
                    pl.BlockSpec(
                        (S + 1, None, None, BLK, BLK), lambda q, p, pos, groups: (0, q, p, 0, 0)
                    )
                ]
                * Z,
                out_specs=[
                    pl.BlockSpec(
                        (Z, 2, None, None, BLK, BLK), lambda q, p, pos, groups: (0, 0, q, p, 0, 0)
                    )
                ]
                * S,
            ),
            out_shape=[jax.ShapeDtypeStruct(out_shape, bf16)] * S,
            name="combine",
        )(pos, groups, *came)

    def within(pieces):
        return [pieces[0]] + [
            lax.ppermute(
                pieces[d], "fsdp", [(z * S + j, z * S + (j ^ d)) for z in range(Z) for j in range(S)]
            )
            for d in range(1, S)
        ]

    quant_shape = (L, R, Z, S, PL, BLK, BLK)
    parity_shape = (2, L, R, Z, S, PL, BLK, BLK)

    def place(chunk, came, quant, parity):
        a, l, q0 = chunk
        held = [v for v in (quant, parity) if v is not None]
        aliases, at = {}, 1 + S
        for slot, v in enumerate((quant, parity)):
            if v is not None:
                aliases[at] = slot
                at += 1
        return pl.pallas_call(
            functools.partial(place_body, S, len(held)),
            grid_spec=pltpu.PrefetchScalarGridSpec(
                num_scalar_prefetch=1,
                grid=(r, Z),
                in_specs=[
                    pl.BlockSpec(
                        (None, 2, None, PL, BLK, BLK), lambda q, z, pos: (z, 0, q, 0, 0, 0)
                    )
                ]
                * S
                + [pl.BlockSpec(memory_space=pl.ANY)] * len(held),
                out_specs=[
                    pl.BlockSpec(
                        (None, None, None, S, PL, BLK, BLK),
                        lambda q, z, pos: (l, q0 + q, z, 0, 0, 0, 0),
                    ),
                    pl.BlockSpec(
                        (None, None, None, None, S, PL, BLK, BLK),
                        lambda q, z, pos: (a, l, q0 + q, z, 0, 0, 0, 0),
                    ),
                ],
            ),
            out_shape=[
                jax.ShapeDtypeStruct(quant_shape, bf16),
                jax.ShapeDtypeStruct(parity_shape, f32),
            ],
            input_output_aliases=aliases,
            name="place",
        )(pos, *came, *held)

    sent, scales = [], []
    for chunk in chunks:
        pieces, scale = quantise(chunk)
        sent.append(across(pieces))
        scales.append(scale)
    quants, parity = [None, None], None
    for chunk, came in zip(chunks, sent):
        arrived = within(combine(came))
        a = chunk[0]
        quants[a], parity = place(chunk, arrived, quants[a], parity)

    table = jnp.stack(scales)
    table = table.transpose(4, 1, 0, 2, 3).reshape(F, len(chunks) * r * PL)
    listed = lax.all_to_all(table, "fsdp", split_axis=0, concat_axis=0, tiled=True)
    listed = listed.reshape(F, L, R // r, 2, r, PL).transpose(3, 1, 2, 4, 0, 5)
    listed = listed.reshape(2, L, R * F * PL)
    blocks = R * F * PL
    return (
        quants[0].reshape(L, blocks, BLK, BLK),
        quants[1].reshape(L, blocks, BLK, BLK),
        listed[0],
        listed[1],
        parity.reshape(1, 2, L, blocks, BLK, BLK),
    )


def solution(mesh):
    in_specs = (P(None, None, "fsdp", "mp", None), P(None, None, "fsdp", "mp", None), P())
    out_specs = (
        P(None, ("fsdp", "mp"), None, None),
        P(None, ("fsdp", "mp"), None, None),
        P(None, ("fsdp", "mp")),
        P(None, ("fsdp", "mp")),
        P(("fsdp", "mp"), None, None, None, None, None),
    )
    return jax.shard_map(shards, mesh=mesh, in_specs=in_specs, out_specs=out_specs, check_vma=False)
```
